1024 devices in a mesh: ctx: 64 (over z, x), ch: 16 (over y, core).
Axes of the slice: x: 4, y: 8, z: 16, core: 2. Of those that a mesh axis runs over, the one named last changes fastest.
Arguments:
- grad_out: bfloat16 [8192, 4096], P('ctx', 'ch'), may hold values from -6 to 6
- out_weight: bfloat16 [4096, 4096], P('ch'), may hold values from -0.09375 to 0.09375
- gate_values: bfloat16 [8192, 4096], P('ctx', 'ch'), may hold values from -6 to 6
- conv_input: bfloat16 [8192, 4096], P('ctx', 'ch'), may hold values from -0.06591797 to 0.06591797
- conv_output: bfloat16 [8192, 4096], P('ctx', 'ch'), may hold values from -6 to 6
- long_filter: float32 [2048, 4096], P('ctx', 'ch'), may hold values from -0.125 to 0.125
- skip_gain: float32 [4096], P('ch'), may hold values from 0.5 to 1.5
Outputs:
- grad_input: bfloat16 [8192, 4096], P('ctx', 'ch')
- grad_gate: bfloat16 [8192, 4096], P('ctx', 'ch')
- grad_filter: float32 [2048, 4096], P('ctx', 'ch')
The draws below stay inside these ranges and needn't reach their ends.
All inputs are finite; a program needn't handle non-finite values.
Results may differ from the reference program's by a relative error of at most 0.0049.
Values may be sent and summed in bfloat16 or wider, within the bound.
No kernel may reach another device: no remote copies, remote signals or barrier semaphores. Data moves between devices by JAX's collectives and lax.ppermute only.
A program may use at most 64 MiB of HBM per device.

```python
import jax
import jax.numpy as jnp

D = 4096
LAG = 2048
TOKENS = 8192


def shard_levels(stream_key, shape, pieces, smallest, largest):
    def one(dim, blocks):
        heights = jax.random.uniform(jax.random.fold_in(jax.random.fold_in(stream_key, 6), dim), (blocks,), jnp.float32, smallest / len(pieces), largest / len(pieces))
        return jnp.repeat(jnp.exp(heights), shape[dim] // blocks).reshape((-1,) + (1,) * (len(shape) - dim - 1))

    gain = one(*pieces[0])
    for cut in pieces[1:]:
        gain = gain * one(*cut)
    return gain


def gaussian(key, extent, spread, most, cuts=(), held_as=jnp.bfloat16):
    drawn = jax.random.normal(key, extent, jnp.float32) * spread
    if len(cuts) > 0:
        drawn = shard_levels(key, extent, cuts, -0.22, 0.18) * drawn
    return jnp.clip(drawn, min=-most, max=most).astype(held_as)


def setup_inputs(seed: int = 0) -> dict:
    arg_keys = jax.random.split(jax.random.key(seed), 8)
    return {
        "grad_out": gaussian(arg_keys[0], (TOKENS, D), 1.0, 6.0, ((0, 64), (1, 16))),
        "out_weight": gaussian(arg_keys[1], (D, D), D ** -0.5, 0.09375, ((0, 16),)),
        "gate_values": gaussian(arg_keys[2], (TOKENS, D), 1.0, 6.0, ((0, 64), (1, 16))),
        "conv_input": gaussian(arg_keys[3], (TOKENS, D), 0.011, 0.06591797, ((0, 64), (1, 16))),
        "conv_output": gaussian(arg_keys[4], (TOKENS, D), 1.0, 6.0, ((0, 64), (1, 16))),
        "long_filter": gaussian(arg_keys[5], (LAG, D), LAG ** -0.5, 0.125, ((0, 64), (1, 16)), jnp.float32),
        "skip_gain": jnp.clip(0.5 + 1.0 * jax.random.uniform(arg_keys[6], (D,), jnp.float32) ** shard_levels(arg_keys[6], (D,), ((0, 16),), -0.2, 0.2), 0.5, 1.5),
    }


def reference(grad_out, out_weight, gate_values, conv_input, conv_output, long_filter, skip_gain):
    dmix = jnp.dot(grad_out, out_weight.T, preferred_element_type=jnp.float32)
    grad_gate = (dmix * conv_output.astype(jnp.float32)).astype(jnp.bfloat16)
    dsignal = (gate_values.astype(jnp.float32) * dmix).astype(jnp.bfloat16)
    signal_full = dsignal.astype(jnp.float32)
    length_total = TOKENS + LAG
    spec_signal = jnp.fft.rfft(signal_full, n=length_total, axis=0)
    spec_filter = jnp.fft.rfft(long_filter, n=length_total, axis=0)
    spec_input = jnp.fft.rfft(conv_input.astype(jnp.float32), n=length_total, axis=0)
    corr = jnp.fft.irfft(jnp.conj(spec_filter) * spec_signal, n=length_total, axis=0)[:TOKENS]
    grad_input = (corr + skip_gain * signal_full).astype(jnp.bfloat16)
    grad_filter = jnp.fft.irfft(spec_signal * jnp.conj(spec_input), n=length_total, axis=0)[:LAG]
    return grad_input, grad_gate, grad_filter.astype(jnp.float32)
```

```python
import functools

import jax
import jax.numpy as jnp
from jax import lax
from jax.experimental import pallas as pl
from jax.experimental.pallas import tpu as pltpu
from jax.sharding import PartitionSpec as P

F32 = jnp.float32
BF16 = jnp.bfloat16
LANES = 128
NT = (((1,), (1,)), ((), ()))

IN_ROWS = 8
OUT_ROWS = 6


def call(body, out_shape, scratch, flops, nbytes):
    return functools.partial(
        pl.pallas_call,
        body,
        out_shape=out_shape,
        scratch_shapes=scratch,
        compiler_params=pltpu.CompilerParams(vmem_limit_bytes=40 * 1024 * 1024),
        cost_estimate=pl.CostEstimate(flops=flops, bytes_accessed=nbytes, transcendentals=0),
    )


def upper(value):
    return value.astype(BF16).astype(F32)


def pack_body(group, conv_ref, taps_ref, out_ref, rows_ref):
    peers, width = rows_ref.shape[0] // IN_ROWS, conv_ref.shape[1]
    turned = conv_ref[...].astype(F32).T
    for j in range(group):
        rows_ref[pl.ds(j, peers, stride=IN_ROWS), :] = turned[j * peers : (j + 1) * peers]
    halves = []
    for start in range(0, width, LANES):
        tile = taps_ref[:, start : start + LANES]
        halves += [tile, pltpu.roll(tile, LANES // 2, 1)]
    taps = jnp.concatenate(halves, axis=0).T[:peers]
    high = upper(taps)
    rows_ref[pl.ds(group, peers, stride=IN_ROWS), :] = high
    rows_ref[pl.ds(group + 1, peers, stride=IN_ROWS), :] = taps - high
    for spare in range(group + 2, IN_ROWS):
        rows_ref[pl.ds(spare, peers, stride=IN_ROWS), :] = jnp.zeros((peers, LANES), F32)
    out_ref[...] = rows_ref[...].astype(BF16)


def gate_body(group, all_ref, weight_ref, gate_ref, conv_ref, grad_gate_ref, out_ref, rows_ref):
    shards, _, depth = all_ref.shape
    peers = rows_ref.shape[0] // group
    dmix = lax.dot_general(all_ref[0], weight_ref[:, :depth], NT, preferred_element_type=F32)
    for s in range(1, shards):
        part = weight_ref[:, s * depth : (s + 1) * depth]
        dmix += lax.dot_general(all_ref[s], part, NT, preferred_element_type=F32)
    grad_gate_ref[...] = (dmix * conv_ref[...].astype(F32)).astype(BF16)
    signal = upper(gate_ref[...].astype(F32) * dmix).T
    for j in range(group):
        rows_ref[pl.ds(j, peers, stride=group), :] = signal[j * peers : (j + 1) * peers]
    out_ref[...] = rows_ref[...].astype(BF16)


def conv_body(
    group, blocks, skip_ref, place_ref, ahead_ref, signal_ref, out_ref,
    ahead_rows, signal_rows, padded, shifted, toeplitz, out_rows,
):
    peers = signal_ref.shape[0] // group
    ahead_rows[...] = ahead_ref[...].astype(F32)
    signal_rows[...] = signal_ref[...].astype(F32)
    row = lax.broadcasted_iota(jnp.int32, (LANES, LANES), 0)
    lane = lax.broadcasted_iota(jnp.int32, (LANES, LANES), 1)
    flip = (row + lane == LANES - 1).astype(BF16)
    below = lane < row
    keep = lane <= row
    tap_lane = lax.broadcasted_iota(jnp.int32, (blocks, LANES), 1) // (LANES // group)
    quarter = LANES // group
    place = place_ref[0]
    tap_rows = []
    for part in range(group):
        high = ahead_rows[pl.ds(part * IN_ROWS + group, blocks, stride=group * IN_ROWS), :]
        low = ahead_rows[pl.ds(part * IN_ROWS + group + 1, blocks, stride=group * IN_ROWS), :]
        tap_rows.append(high + low)
    padded[peers:, :] = jnp.zeros((padded.shape[0] - peers, LANES), F32)
    lag_rows = []
    for j in range(group):
        signal = signal_rows[pl.ds(j, peers, stride=group), :]
        conv = ahead_rows[pl.ds(j, peers, stride=IN_ROWS), :].astype(BF16)
        padded[:peers, :] = signal
        for k in range(blocks + 1):
            shifted[:, k * LANES : (k + 1) * LANES] = padded[k : k + peers, :].astype(BF16)
        taps = jnp.zeros((blocks, LANES), F32)
        for part in range(group):
            moved = pltpu.roll(tap_rows[part], (part - j) % group * quarter, 1)
            taps = jnp.where(tap_lane == part, moved, taps)
        before = jnp.zeros((LANES, LANES), F32)
        for k in range(blocks + 1):
            if k < blocks:
                spread = jnp.broadcast_to(taps[k : k + 1, :], (LANES, LANES))
                now = pltpu.roll(spread, 0, 1, stride=1, stride_axis=0)
            else:
                now = jnp.zeros((LANES, LANES), F32)
            both = jnp.where(below, before, now)
            high = both.astype(BF16)
            toeplitz[:LANES, k * LANES : (k + 1) * LANES] = high
            toeplitz[LANES:, k * LANES : (k + 1) * LANES] = (both - high.astype(F32)).astype(BF16)
            before = now
        corr = lax.dot_general(toeplitz[...], shifted[...], NT, preferred_element_type=F32)
        corr = (corr[:LANES] + corr[LANES:]).T
        gain = skip_ref[j * peers + place]
        out_rows[pl.ds(j, peers, stride=OUT_ROWS), :] = corr + gain * signal
        turned = lax.dot_general(flip, conv, NT, preferred_element_type=F32).astype(BF16)
        products = jnp.dot(turned, shifted[...], preferred_element_type=F32)
        sums = []
        now = pltpu.roll(products[:, :LANES], 1, 1, stride=1, stride_axis=0)
        for k in range(blocks):
            later = pltpu.roll(
                products[:, (k + 1) * LANES : (k + 2) * LANES], 1, 1, stride=1, stride_axis=0
            )
            sums.append(jnp.sum(jnp.where(keep, now, later), axis=0, keepdims=True))
            now = later
        lag_rows.append(jnp.concatenate(sums, axis=0))
    for part in range(group):
        mine = jnp.zeros((blocks, LANES), F32)
        for j in range(group):
            moved = pltpu.roll(lag_rows[j], (j - part) % group * quarter, 1)
            mine = jnp.where(tap_lane == j, moved, mine)
        high = upper(mine)
        out_rows[pl.ds(part * OUT_ROWS + group, blocks, stride=group * OUT_ROWS), :] = high
        out_rows[pl.ds(part * OUT_ROWS + group + 1, blocks, stride=group * OUT_ROWS), :] = mine - high
    out_ref[...] = out_rows[...].astype(BF16)


def unpack_body(group, back_ref, grad_input_ref, grad_filter_ref, rows_ref):
    peers = rows_ref.shape[0] // OUT_ROWS
    rows_ref[...] = back_ref[...].astype(F32)
    parts = [rows_ref[pl.ds(j, peers, stride=OUT_ROWS), :] for j in range(group)]
    grad_input_ref[...] = jnp.concatenate(parts, axis=0).T.astype(BF16)
    lags = rows_ref[pl.ds(group, peers, stride=OUT_ROWS), :] + rows_ref[pl.ds(group + 1, peers, stride=OUT_ROWS), :]
    turned = jnp.concatenate([lags, lags], axis=0).T
    quarter = LANES // group
    left = lax.broadcasted_iota(jnp.int32, (quarter, LANES), 1) < peers
    for pair in range(group // 2):
        even = turned[2 * pair * quarter : (2 * pair + 1) * quarter]
        odd = turned[(2 * pair + 1) * quarter : (2 * pair + 2) * quarter]
        grad_filter_ref[:, pair * LANES : (pair + 1) * LANES] = jnp.where(left, even, odd)


def local(grad_out, out_weight, gate_values, conv_input, conv_output, long_filter, skip_gain):
    tok_rows, chan_width = conv_input.shape
    peers = lax.axis_size("ctx")
    group = chan_width // peers
    lag_rows = long_filter.shape[0]
    blocks = lag_rows * peers // tok_rows
    place = lax.axis_index("ctx").astype(jnp.int32).reshape(1)
    vmem = pltpu.VMEM
    shape = jax.ShapeDtypeStruct

    gathered = lax.all_gather(grad_out, "ch", axis=0, tiled=False)

    ahead = call(
        functools.partial(pack_body, group),
        shape((peers * IN_ROWS, tok_rows), BF16),
        [vmem((peers * IN_ROWS, tok_rows), F32)],
        0,
        200_000,
    )()(conv_input, long_filter)
    ahead = lax.all_to_all(ahead.reshape(peers, IN_ROWS, tok_rows), "ctx", 0, 0, tiled=True)

    grad_gate, signal = call(
        functools.partial(gate_body, group),
        (shape((tok_rows, chan_width), BF16), shape((chan_width, tok_rows), BF16)),
        [vmem((chan_width, tok_rows), F32)],
        2 * tok_rows * out_weight.size,
        2 * out_weight.size,
    )()(gathered, out_weight, gate_values, conv_output)
    signal = lax.all_to_all(signal.reshape(peers, group, tok_rows), "ctx", 0, 0, tiled=True)

    span = (blocks + 1) * tok_rows
    smem = pl.BlockSpec(memory_space=pltpu.SMEM)
    whole = pl.BlockSpec(memory_space=pltpu.VMEM)
    back = call(
        functools.partial(conv_body, group, blocks),
        shape((peers * OUT_ROWS, tok_rows), BF16),
        [
            vmem((peers * IN_ROWS, tok_rows), F32),
            vmem((peers * group, tok_rows), F32),
            vmem((peers + blocks, tok_rows), F32),
            vmem((peers, span), BF16),
            vmem((2 * tok_rows, span), BF16),
            vmem((peers * OUT_ROWS, tok_rows), F32),
        ],
        6 * group * peers * tok_rows * span,
        1_000_000,
    )(in_specs=[smem, smem, whole, whole])(
        skip_gain,
        place,
        ahead.reshape(peers * IN_ROWS, tok_rows),
        signal.reshape(peers * group, tok_rows),
    )
    back = lax.all_to_all(back.reshape(peers, OUT_ROWS, tok_rows), "ctx", 0, 0, tiled=True)
    grad_input, grad_filter = call(
        functools.partial(unpack_body, group),
        (shape((tok_rows, chan_width), BF16), shape((lag_rows, chan_width), F32)),
        [vmem((peers * OUT_ROWS, tok_rows), F32)],
        0,
        300_000,
    )()(back.reshape(peers * OUT_ROWS, tok_rows))
    return grad_input, grad_gate, grad_filter


def solution(mesh):
    in_specs = (
        P("ctx", "ch"),
        P("ch", None),
        P("ctx", "ch"),
        P("ctx", "ch"),
        P("ctx", "ch"),
        P("ctx", "ch"),
        P("ch"),
    )
    out_specs = (P("ctx", "ch"), P("ctx", "ch"), P("ctx", "ch"))
    return jax.shard_map(local, mesh=mesh, in_specs=in_specs, out_specs=out_specs, check_vma=False)
```

```python
import functools

import jax
import jax.numpy as jnp
from jax import lax
from jax.experimental import pallas as pl
from jax.experimental.pallas import tpu as pltpu
from jax.sharding import PartitionSpec as P

F32 = jnp.float32
BF16 = jnp.bfloat16
LANES = 128
NT = (((1,), (1,)), ((), ()))

IN_ROWS = 10
OUT_ROWS = 6


def call(body, out_shape, scratch, flops, nbytes):
    return functools.partial(
        pl.pallas_call,
        body,
        out_shape=out_shape,
        scratch_shapes=scratch,
        compiler_params=pltpu.CompilerParams(vmem_limit_bytes=40 * 1024 * 1024),
        cost_estimate=pl.CostEstimate(flops=flops, bytes_accessed=nbytes, transcendentals=0),
    )


def upper(value):
    return value.astype(BF16).astype(F32)


def first_body(
    group, core_ref, mine_ref, weight_hbm, gate_hbm, conv_out_hbm, conv_hbm, taps_hbm,
    part_ref, weight_ref, gate_ref, conv_out_ref, conv_turned_ref, taps_ref,
    weight_mine, conv_here, taps_here, mine_sems, other_sems, sems,
):
    chips, _, depth = mine_ref.shape
    peers = taps_ref.shape[1]
    width = conv_here.shape[1]
    core = core_ref[0]

    def columns(parity, chip, target, sem):
        first = pl.multiple_of((2 * chip + parity) * depth, depth)
        inside = target.at[:, chip * depth : (chip + 1) * depth]
        return pltpu.make_async_copy(weight_hbm.at[:, pl.ds(first, depth)], inside, sem.at[chip])

    mine = [columns(core, chip, weight_mine, mine_sems) for chip in range(chips)]
    small = [
        pltpu.make_async_copy(conv_hbm, conv_here, sems.at[0]),
        pltpu.make_async_copy(taps_hbm, taps_here, sems.at[1]),
        pltpu.make_async_copy(gate_hbm, gate_ref, sems.at[2]),
        pltpu.make_async_copy(conv_out_hbm, conv_out_ref, sems.at[3]),
    ]
    other = [columns(1 - core, chip, weight_ref, other_sems) for chip in range(chips)]
    for copy in small[:2] + mine + small[2:] + other:
        copy.start()
    small[0].wait()
    conv_turned_ref[...] = conv_here[...].astype(F32).T
    small[1].wait()
    halves = []
    for start in range(0, width, LANES):
        tile = taps_here[:, start : start + LANES]
        halves += [tile, pltpu.roll(tile, LANES // 2, 1)]
    taps = jnp.concatenate(halves, axis=0).T[:peers]
    high = upper(taps)
    taps_ref[0] = high
    taps_ref[1] = taps - high
    total = None
    for chip in range(chips):
        mine[chip].wait()
        part = weight_mine[:, chip * depth : (chip + 1) * depth]
        term = lax.dot_general(mine_ref[chip], part, NT, preferred_element_type=F32)
        total = term if total is None else total + term
    part_ref[...] = total
    for copy in small[2:] + other:
        copy.wait()


def second_body(
    group, other_ref, part_ref, weight_ref, gate_ref, conv_out_ref, conv_turned_ref, taps_ref,
    grad_gate_ref, out_ref, rows_ref,
):
    chips, _, depth = other_ref.shape
    peers = rows_ref.shape[0] // IN_ROWS
    dmix = part_ref[...]
    for chip in range(chips):
        part = weight_ref[:, chip * depth : (chip + 1) * depth]
        dmix += lax.dot_general(other_ref[chip], part, NT, preferred_element_type=F32)
    grad_gate_ref[...] = (dmix * conv_out_ref[...].astype(F32)).astype(BF16)
    signal = upper(gate_ref[...].astype(F32) * dmix).T
    for j in range(group):
        rows_ref[pl.ds(j, peers, stride=IN_ROWS), :] = conv_turned_ref[j * peers : (j + 1) * peers]
        rows_ref[pl.ds(group + 2 + j, peers, stride=IN_ROWS), :] = signal[j * peers : (j + 1) * peers]
    rows_ref[pl.ds(group, peers, stride=IN_ROWS), :] = taps_ref[0]
    rows_ref[pl.ds(group + 1, peers, stride=IN_ROWS), :] = taps_ref[1]
    out_ref[...] = rows_ref[...].astype(BF16)


def conv_body(
    group, blocks, skip_ref, place_ref, in_ref, out_ref,
    in_rows, padded, shifted, toeplitz, out_rows,
):
    peers = in_rows.shape[0] // IN_ROWS
    in_rows[...] = in_ref[...].astype(F32)
    row = lax.broadcasted_iota(jnp.int32, (LANES, LANES), 0)
    lane = lax.broadcasted_iota(jnp.int32, (LANES, LANES), 1)
    flip = (row + lane == LANES - 1).astype(BF16)
    below = lane < row
    keep = lane <= row
    tap_lane = lax.broadcasted_iota(jnp.int32, (blocks, LANES), 1) // (LANES // group)
    quarter = LANES // group
    place = place_ref[0]
    tap_rows = []
    for part in range(group):
        high = in_rows[pl.ds(part * IN_ROWS + group, blocks, stride=group * IN_ROWS), :]
        low = in_rows[pl.ds(part * IN_ROWS + group + 1, blocks, stride=group * IN_ROWS), :]
        tap_rows.append(high + low)
    padded[peers:, :] = jnp.zeros((padded.shape[0] - peers, LANES), F32)
    lag_rows = []
    for j in range(group):
        signal = in_rows[pl.ds(group + 2 + j, peers, stride=IN_ROWS), :]
        conv = in_rows[pl.ds(j, peers, stride=IN_ROWS), :].astype(BF16)
        padded[:peers, :] = signal
        for k in range(blocks + 1):
            shifted[:, k * LANES : (k + 1) * LANES] = padded[k : k + peers, :].astype(BF16)
        taps = jnp.zeros((blocks, LANES), F32)
        for part in range(group):
            moved = pltpu.roll(tap_rows[part], (part - j) % group * quarter, 1)
            taps = jnp.where(tap_lane == part, moved, taps)
        before = jnp.zeros((LANES, LANES), F32)
        for k in range(blocks + 1):
            if k < blocks:
                spread = jnp.broadcast_to(taps[k : k + 1, :], (LANES, LANES))
                now = pltpu.roll(spread, 0, 1, stride=1, stride_axis=0)
            else:
                now = jnp.zeros((LANES, LANES), F32)
            both = jnp.where(below, before, now)
            high = both.astype(BF16)
            toeplitz[:LANES, k * LANES : (k + 1) * LANES] = high
            toeplitz[LANES:, k * LANES : (k + 1) * LANES] = (both - high.astype(F32)).astype(BF16)
            before = now
        corr = lax.dot_general(toeplitz[...], shifted[...], NT, preferred_element_type=F32)
        corr = (corr[:LANES] + corr[LANES:]).T
        gain = skip_ref[j * peers + place]
        out_rows[pl.ds(j, peers, stride=OUT_ROWS), :] = corr + gain * signal
        turned = lax.dot_general(flip, conv, NT, preferred_element_type=F32).astype(BF16)
        products = jnp.dot(turned, shifted[...], preferred_element_type=F32)
        sums = []
        now = pltpu.roll(products[:, :LANES], 1, 1, stride=1, stride_axis=0)
        for k in range(blocks):
            later = pltpu.roll(
                products[:, (k + 1) * LANES : (k + 2) * LANES], 1, 1, stride=1, stride_axis=0
            )
            sums.append(jnp.sum(jnp.where(keep, now, later), axis=0, keepdims=True))
            now = later
        lag_rows.append(jnp.concatenate(sums, axis=0))
    for part in range(group):
        mine = jnp.zeros((blocks, LANES), F32)
        for j in range(group):
            moved = pltpu.roll(lag_rows[j], (j - part) % group * quarter, 1)
            mine = jnp.where(tap_lane == j, moved, mine)
        high = upper(mine)
        out_rows[pl.ds(part * OUT_ROWS + group, blocks, stride=group * OUT_ROWS), :] = high
        out_rows[pl.ds(part * OUT_ROWS + group + 1, blocks, stride=group * OUT_ROWS), :] = mine - high
    out_ref[...] = out_rows[...].astype(BF16)


def unpack_body(group, back_ref, grad_input_ref, grad_filter_ref, rows_ref):
    peers = rows_ref.shape[0] // OUT_ROWS
    rows_ref[...] = back_ref[...].astype(F32)
    parts = [rows_ref[pl.ds(j, peers, stride=OUT_ROWS), :] for j in range(group)]
    grad_input_ref[...] = jnp.concatenate(parts, axis=0).T.astype(BF16)
    lags = rows_ref[pl.ds(group, peers, stride=OUT_ROWS), :] + rows_ref[pl.ds(group + 1, peers, stride=OUT_ROWS), :]
    turned = jnp.concatenate([lags, lags], axis=0).T
    quarter = LANES // group
    left = lax.broadcasted_iota(jnp.int32, (quarter, LANES), 1) < peers
    for pair in range(group // 2):
        even = turned[2 * pair * quarter : (2 * pair + 1) * quarter]
        odd = turned[(2 * pair + 1) * quarter : (2 * pair + 2) * quarter]
        grad_filter_ref[:, pair * LANES : (pair + 1) * LANES] = jnp.where(left, even, odd)


def exchange(rows, count):
    peers = lax.axis_size("ctx")
    pairs = rows.reshape(peers, count // 2, 2, rows.shape[1])
    return lax.all_to_all(pairs, "ctx", 0, 0, tiled=True).reshape(rows.shape)


def local(grad_out, out_weight, gate_values, conv_input, conv_output, long_filter, skip_gain):
    tok_rows, chan_width = conv_input.shape
    peers = lax.axis_size("ctx")
    group = chan_width // peers
    lag_rows = long_filter.shape[0]
    blocks = lag_rows * peers // tok_rows
    place = lax.axis_index("ctx").astype(jnp.int32).reshape(1)
    vmem = pltpu.VMEM
    shape = jax.ShapeDtypeStruct
    smem = pl.BlockSpec(memory_space=pltpu.SMEM)
    whole = pl.BlockSpec(memory_space=pltpu.VMEM)

    chips = lax.axis_size("ch") // 2
    core = (lax.axis_index("ch") % 2).astype(jnp.int32).reshape(1)
    sides = [[2 * chip + side for chip in range(chips)] for side in range(2)]
    copies = jnp.broadcast_to(grad_out[None], (chips, tok_rows, chan_width))
    mine = lax.all_to_all(copies, "ch", 0, 0, tiled=True, axis_index_groups=sides)
    other = lax.ppermute(mine, "ch", [(i, i ^ 1) for i in range(2 * chips)])

    hbm = pl.BlockSpec(memory_space=pltpu.HBM)
    dma = pltpu.SemaphoreType.DMA
    half = chips * chan_width
    local_shape = (tok_rows, chan_width)
    stored = (out_weight, gate_values, conv_output, conv_input, long_filter)
    ready = call(
        functools.partial(first_body, group),
        (
            shape(local_shape, F32),
            shape((chan_width, half), BF16),
            shape(local_shape, BF16),
            shape(local_shape, BF16),
            shape((chan_width, tok_rows), F32),
            shape((2, peers, tok_rows), F32),
        ),
        [
            vmem((chan_width, half), BF16),
            vmem(local_shape, BF16),
            vmem((lag_rows, chan_width), F32),
            dma((chips,)),
            dma((chips,)),
            dma((4,)),
        ],
        tok_rows * out_weight.size,
        2 * out_weight.size,
    )(in_specs=[smem, whole] + [hbm] * 5)(
        core, mine, *(pltpu.with_memory_space_constraint(held, pltpu.HBM) for held in stored)
    )
    grad_gate, rows = call(
        functools.partial(second_body, group),
        (shape(local_shape, BF16), shape((peers * IN_ROWS, tok_rows), BF16)),
        [vmem((peers * IN_ROWS, tok_rows), F32)],
        tok_rows * out_weight.size,
        2 * out_weight.size,
    )()(other, *ready)
    rows = exchange(rows, IN_ROWS)

    span = (blocks + 1) * tok_rows
    back = call(
        functools.partial(conv_body, group, blocks),
        shape((peers * OUT_ROWS, tok_rows), BF16),
        [
            vmem((peers * IN_ROWS, tok_rows), F32),
            vmem((peers + blocks, tok_rows), F32),
            vmem((peers, span), BF16),
            vmem((2 * tok_rows, span), BF16),
            vmem((peers * OUT_ROWS, tok_rows), F32),
        ],
        6 * group * peers * tok_rows * span,
        1_000_000,
    )(in_specs=[smem, smem, whole])(skip_gain, place, rows)
    back = exchange(back, OUT_ROWS)
    grad_input, grad_filter = call(
        functools.partial(unpack_body, group),
        (shape((tok_rows, chan_width), BF16), shape((lag_rows, chan_width), F32)),
        [vmem((peers * OUT_ROWS, tok_rows), F32)],
        0,
        300_000,
    )()(back)
    return grad_input, grad_gate, grad_filter


def solution(mesh):
    in_specs = (
        P("ctx", "ch"),
        P("ch", None),
        P("ctx", "ch"),
        P("ctx", "ch"),
        P("ctx", "ch"),
        P("ctx", "ch"),
        P("ch"),
    )
    out_specs = (P("ctx", "ch"), P("ctx", "ch"), P("ctx", "ch"))
    return jax.shard_map(local, mesh=mesh, in_specs=in_specs, out_specs=out_specs, check_vma=False)
```

```python
import functools

import jax
import jax.numpy as jnp
from jax import lax
from jax.experimental import pallas as pl
from jax.experimental.pallas import tpu as pltpu
from jax.sharding import PartitionSpec as P

F32 = jnp.float32
BF16 = jnp.bfloat16
LANES = 128
PART = 64
NT = (((1,), (1,)), ((), ()))

IN_ROWS = 10
OUT_ROWS = 6


def call(body, out_shape, scratch, flops, nbytes):
    return functools.partial(
        pl.pallas_call,
        body,
        out_shape=out_shape,
        scratch_shapes=scratch,
        compiler_params=pltpu.CompilerParams(vmem_limit_bytes=40 * 1024 * 1024),
        cost_estimate=pl.CostEstimate(flops=flops, bytes_accessed=nbytes, transcendentals=0),
    )


def upper(value):
    return value.astype(BF16).astype(F32)


def first_body(
    group, core_ref, mine_ref, weight_hbm, gate_hbm, conv_out_hbm, conv_hbm, taps_hbm,
    part_ref, weight_ref, gate_ref, conv_out_ref, conv_turned_ref, taps_ref,
    weight_mine, conv_here, taps_here, mine_sems, other_sems, sems,
):
    chips, _, depth = mine_ref.shape
    peers = taps_ref.shape[1]
    width = conv_here.shape[1]
    core = core_ref[0]

    def columns(parity, chip, target, sem):
        first = pl.multiple_of((2 * chip + parity) * depth, depth)
        inside = target.at[:, chip * depth : (chip + 1) * depth]
        return pltpu.make_async_copy(weight_hbm.at[:, pl.ds(first, depth)], inside, sem.at[chip])

    mine = [columns(core, chip, weight_mine, mine_sems) for chip in range(chips)]
    small = [
        pltpu.make_async_copy(conv_hbm, conv_here, sems.at[0]),
        pltpu.make_async_copy(taps_hbm, taps_here, sems.at[1]),
        pltpu.make_async_copy(gate_hbm, gate_ref, sems.at[2]),
        pltpu.make_async_copy(conv_out_hbm, conv_out_ref, sems.at[3]),
    ]
    other = [columns(1 - core, chip, weight_ref, other_sems) for chip in range(chips)]
    for copy in small[:2] + mine + small[2:] + other:
        copy.start()
    small[0].wait()
    conv_turned_ref[...] = conv_here[...].astype(F32).T
    small[1].wait()
    halves = []
    for start in range(0, width, LANES):
        tile = taps_here[:, start : start + LANES]
        halves += [tile, pltpu.roll(tile, LANES // 2, 1)]
    taps = jnp.concatenate(halves, axis=0).T[:peers]
    high = upper(taps)
    taps_ref[0] = high
    taps_ref[1] = taps - high
    total = None
    step = chips // 2
    for start in range(0, chips, step):
        some = range(start, start + step)
        for chip in some:
            mine[chip].wait()
        rows = jnp.concatenate([mine_ref[chip] for chip in some], axis=1)
        part = weight_mine[:, start * depth : (start + step) * depth]
        term = lax.dot_general(rows, part, NT, preferred_element_type=F32)
        total = term if total is None else total + term
    part_ref[...] = total
    for copy in small[2:] + other:
        copy.wait()


def second_body(
    group, other_ref, part_ref, weight_ref, gate_ref, conv_out_ref, conv_turned_ref, taps_ref,
    grad_gate_ref, out_ref, rows_ref,
):
    chips = other_ref.shape[0]
    peers = rows_ref.shape[0] // IN_ROWS
    rows = jnp.concatenate([other_ref[chip] for chip in range(chips)], axis=1)
    dmix = part_ref[...] + lax.dot_general(rows, weight_ref[...], NT, preferred_element_type=F32)
    grad_gate_ref[...] = (dmix * conv_out_ref[...].astype(F32)).astype(BF16)
    signal = upper(gate_ref[...].astype(F32) * dmix).T
    for j in range(group):
        rows_ref[pl.ds(j, peers, stride=IN_ROWS), :] = conv_turned_ref[j * peers : (j + 1) * peers]
        rows_ref[pl.ds(group + 2 + j, peers, stride=IN_ROWS), :] = signal[j * peers : (j + 1) * peers]
    rows_ref[pl.ds(group, peers, stride=IN_ROWS), :] = taps_ref[0]
    rows_ref[pl.ds(group + 1, peers, stride=IN_ROWS), :] = taps_ref[1]
    out_ref[...] = rows_ref[...].astype(BF16)


def conv_body(
    group, blocks, skip_ref, place_ref, in_ref, out_ref,
    in_rows, padded, moved_rows, spans, taps_spans, out_rows,
):
    peers = in_rows.shape[0] // IN_ROWS
    parts = LANES // PART
    in_rows[...] = in_ref[...].astype(F32)
    row = lax.broadcasted_iota(jnp.int32, (LANES, LANES), 0)
    lane = lax.broadcasted_iota(jnp.int32, (LANES, LANES), 1)
    flip = (row + lane == LANES - 1).astype(BF16)
    below = (lane < row)[:PART]
    keep = (lane <= row + (LANES - PART))[:PART]
    left = (lane < peers)[:PART]
    rows_lane = lax.broadcasted_iota(jnp.int32, (peers + blocks, LANES), 1)
    tap_lane = lax.broadcasted_iota(jnp.int32, (blocks, LANES), 1) // (LANES // group)
    quarter = LANES // group
    place = place_ref[0]
    tap_rows = []
    for part in range(group):
        high = in_rows[pl.ds(part * IN_ROWS + group, blocks, stride=group * IN_ROWS), :]
        low = in_rows[pl.ds(part * IN_ROWS + group + 1, blocks, stride=group * IN_ROWS), :]
        tap_rows.append(high + low)
    lag_rows = []
    for j in range(group):
        signal = in_rows[pl.ds(group + 2 + j, peers, stride=IN_ROWS), :]
        conv = in_rows[pl.ds(j, peers, stride=IN_ROWS), :].astype(BF16)
        padded[j, :peers, :] = signal
        padded[j, peers:, :] = jnp.zeros((padded.shape[1] - peers, LANES), F32)
        for a in range(parts):
            if a > 0:
                turned = pltpu.roll(padded[j], LANES - a * PART, 1)
                moved_rows[j] = turned
                here = moved_rows[j, : peers + blocks, :]
                following = moved_rows[j, 1 : peers + blocks + 1, :]
                padded_a = jnp.where(rows_lane < LANES - a * PART, here, following)
                moved_rows[j, : peers + blocks, :] = padded_a
            source = padded if a == 0 else moved_rows
            for k in range(blocks + 1):
                rows = source[j, k : k + peers, :].astype(BF16)
                spans[j, a * peers : (a + 1) * peers, k * LANES : (k + 1) * LANES] = rows
        taps = jnp.zeros((blocks, LANES), F32)
        for part in range(group):
            moved = pltpu.roll(tap_rows[part], (part - j) % group * quarter, 1)
            taps = jnp.where(tap_lane == part, moved, taps)
        before = jnp.zeros((PART, LANES), F32)
        for k in range(blocks + 1):
            if k < blocks:
                spread = jnp.broadcast_to(taps[k : k + 1, :], (PART, LANES))
                now = pltpu.roll(spread, 0, 1, stride=1, stride_axis=0)
            else:
                now = jnp.zeros((PART, LANES), F32)
            both = jnp.where(below, before, now)
            high = both.astype(BF16)
            taps_spans[j, :PART, k * LANES : (k + 1) * LANES] = high
            taps_spans[j, PART:, k * LANES : (k + 1) * LANES] = (both - high.astype(F32)).astype(BF16)
            before = now
        corr = lax.dot_general(taps_spans[j], spans[j], NT, preferred_element_type=F32)
        corr = corr[:PART] + corr[PART:]
        stacked = []
        for a in range(0, parts, 2):
            pair = corr[:, a * peers : (a + 2) * peers]
            stacked += [pair, pltpu.roll(pair, peers, 1)]
        corr = jnp.concatenate(stacked, axis=0).T[:peers]
        gain = skip_ref[j * peers + place]
        out_rows[pl.ds(j, peers, stride=OUT_ROWS), :] = corr + gain * signal
        twice = jnp.concatenate([conv, conv], axis=0)
        turned = lax.dot_general(flip, twice, NT, preferred_element_type=F32)
        pairs = []
        for a in range(0, parts, 2):
            even = turned[LANES - (a + 1) * PART : LANES - a * PART]
            odd = turned[LANES - (a + 2) * PART : LANES - (a + 1) * PART]
            pairs.append(jnp.where(left, even, odd).astype(BF16))
        factors = pairs[0] if len(pairs) == 1 else jnp.concatenate(pairs, axis=1)
        products = jnp.dot(factors, spans[j], preferred_element_type=F32)
        sums = []
        first = LANES + 1 - PART
        now = pltpu.roll(products[:, :LANES], first, 1, stride=1, stride_axis=0)
        for k in range(blocks):
            tile = products[:, (k + 1) * LANES : (k + 2) * LANES]
            later = pltpu.roll(tile, first, 1, stride=1, stride_axis=0)
            sums.append(jnp.sum(jnp.where(keep, now, later), axis=0, keepdims=True))
            now = later
        lag_rows.append(jnp.concatenate(sums, axis=0))
    for part in range(group):
        mine = jnp.zeros((blocks, LANES), F32)
        for j in range(group):
            moved = pltpu.roll(lag_rows[j], (j - part) % group * quarter, 1)
            mine = jnp.where(tap_lane == j, moved, mine)
        high = upper(mine)
        out_rows[pl.ds(part * OUT_ROWS + group, blocks, stride=group * OUT_ROWS), :] = high
        out_rows[pl.ds(part * OUT_ROWS + group + 1, blocks, stride=group * OUT_ROWS), :] = mine - high
    out_ref[...] = out_rows[...].astype(BF16)


def unpack_body(group, back_ref, grad_input_ref, grad_filter_ref, rows_ref):
    peers = rows_ref.shape[0] // OUT_ROWS
    rows_ref[...] = back_ref[...].astype(F32)
    parts = [rows_ref[pl.ds(j, peers, stride=OUT_ROWS), :] for j in range(group)]
    grad_input_ref[...] = jnp.concatenate(parts, axis=0).T.astype(BF16)
    lags = rows_ref[pl.ds(group, peers, stride=OUT_ROWS), :] + rows_ref[pl.ds(group + 1, peers, stride=OUT_ROWS), :]
    turned = jnp.concatenate([lags, lags], axis=0).T
    quarter = LANES // group
    left = lax.broadcasted_iota(jnp.int32, (quarter, LANES), 1) < peers
    for pair in range(group // 2):
        even = turned[2 * pair * quarter : (2 * pair + 1) * quarter]
        odd = turned[(2 * pair + 1) * quarter : (2 * pair + 2) * quarter]
        grad_filter_ref[:, pair * LANES : (pair + 1) * LANES] = jnp.where(left, even, odd)


def exchange(rows, count):
    peers = lax.axis_size("ctx")
    pairs = rows.reshape(peers, count // 2, 2, rows.shape[1])
    return lax.all_to_all(pairs, "ctx", 0, 0, tiled=True).reshape(rows.shape)


def local(grad_out, out_weight, gate_values, conv_input, conv_output, long_filter, skip_gain):
    tok_rows, chan_width = conv_input.shape
    peers = lax.axis_size("ctx")
    group = chan_width // peers
    lag_rows = long_filter.shape[0]
    blocks = lag_rows * peers // tok_rows
    place = lax.axis_index("ctx").astype(jnp.int32).reshape(1)
    vmem = pltpu.VMEM
    shape = jax.ShapeDtypeStruct
    smem = pl.BlockSpec(memory_space=pltpu.SMEM)
    whole = pl.BlockSpec(memory_space=pltpu.VMEM)

    chips = lax.axis_size("ch") // 2
    core = (lax.axis_index("ch") % 2).astype(jnp.int32).reshape(1)
    core, place = lax.optimization_barrier((core, place))
    sides = [[2 * chip + side for chip in range(chips)] for side in range(2)]
    copies = jnp.broadcast_to(grad_out[None], (chips, tok_rows, chan_width))
    mine = lax.all_to_all(copies, "ch", 0, 0, tiled=True, axis_index_groups=sides)
    other = lax.ppermute(mine, "ch", [(i, i ^ 1) for i in range(2 * chips)])

    hbm = pl.BlockSpec(memory_space=pltpu.HBM)
    dma = pltpu.SemaphoreType.DMA
    half = chips * chan_width
    local_shape = (tok_rows, chan_width)
    stored = (out_weight, gate_values, conv_output, conv_input, long_filter)
    ready = call(
        functools.partial(first_body, group),
        (
            shape(local_shape, F32),
            shape((chan_width, half), BF16),
            shape(local_shape, BF16),
            shape(local_shape, BF16),
            shape((chan_width, tok_rows), F32),
            shape((2, peers, tok_rows), F32),
        ),
        [
            vmem((chan_width, half), BF16),
            vmem(local_shape, BF16),
            vmem((lag_rows, chan_width), F32),
            dma((chips,)),
            dma((chips,)),
            dma((4,)),
        ],
        tok_rows * out_weight.size,
        2 * out_weight.size,
    )(in_specs=[smem, whole] + [hbm] * 5)(
        core, mine, *(pltpu.with_memory_space_constraint(held, pltpu.HBM) for held in stored)
    )
    grad_gate, rows = call(
        functools.partial(second_body, group),
        (shape(local_shape, BF16), shape((peers * IN_ROWS, tok_rows), BF16)),
        [vmem((peers * IN_ROWS, tok_rows), F32)],
        tok_rows * out_weight.size,
        2 * out_weight.size,
    )()(other, *ready)
    rows = exchange(rows, IN_ROWS)

    span = (blocks + 1) * tok_rows
    back = call(
        functools.partial(conv_body, group, blocks),
        shape((peers * OUT_ROWS, tok_rows), BF16),
        [
            vmem((peers * IN_ROWS, tok_rows), F32),
            vmem((group, peers + blocks + 8, tok_rows), F32),
            vmem((group, peers + blocks + 8, tok_rows), F32),
            vmem((group, peers * (tok_rows // PART), span), BF16),
            vmem((group, 2 * PART, span), BF16),
            vmem((peers * OUT_ROWS, tok_rows), F32),
        ],
        6 * group * peers * tok_rows * span,
        1_000_000,
    )(in_specs=[smem, smem, whole])(skip_gain, place, rows)
    back = exchange(back, OUT_ROWS)
    grad_input, grad_filter = call(
        functools.partial(unpack_body, group),
        (shape((tok_rows, chan_width), BF16), shape((lag_rows, chan_width), F32)),
        [vmem((peers * OUT_ROWS, tok_rows), F32)],
        0,
        300_000,
    )()(back)
    return grad_input, grad_gate, grad_filter


def solution(mesh):
    in_specs = (
        P("ctx", "ch"),
        P("ch", None),
        P("ctx", "ch"),
        P("ctx", "ch"),
        P("ctx", "ch"),
        P("ctx", "ch"),
        P("ch"),
    )
    out_specs = (P("ctx", "ch"), P("ctx", "ch"), P("ctx", "ch"))
    return jax.shard_map(local, mesh=mesh, in_specs=in_specs, out_specs=out_specs, check_vma=False)
```

```python
import functools

import jax
import jax.numpy as jnp
from jax import lax
from jax.experimental import pallas as pl
from jax.experimental.pallas import tpu as pltpu
from jax.sharding import PartitionSpec as P

F32 = jnp.float32
BF16 = jnp.bfloat16
LANES = 128
PART = 64
NT = (((1,), (1,)), ((), ()))

IN_ROWS = 10
OUT_ROWS = 6


def call(body, out_shape, scratch, flops, nbytes):
    return functools.partial(
        pl.pallas_call,
        body,
        out_shape=out_shape,
        scratch_shapes=scratch,
        compiler_params=pltpu.CompilerParams(vmem_limit_bytes=40 * 1024 * 1024),
        cost_estimate=pl.CostEstimate(flops=flops, bytes_accessed=nbytes, transcendentals=0),
    )


def upper(value):
    return value.astype(BF16).astype(F32)


def first_body(
    group, core_ref, mine_ref, weight_hbm, conv_hbm, taps_hbm, part_ref, conv_turned_ref, taps_ref,
    weight_mine, conv_here, taps_here, mine_sems, sems,
):
    chips, _, depth = mine_ref.shape
    peers = taps_ref.shape[1]
    width = conv_here.shape[1]
    core = core_ref[0]

    def columns(parity, chip, target, sem):
        first = pl.multiple_of((2 * chip + parity) * depth, depth)
        inside = target.at[:, chip * depth : (chip + 1) * depth]
        return pltpu.make_async_copy(weight_hbm.at[:, pl.ds(first, depth)], inside, sem.at[chip])

    mine = [columns(core, chip, weight_mine, mine_sems) for chip in range(chips)]
    small = [
        pltpu.make_async_copy(conv_hbm, conv_here, sems.at[0]),
        pltpu.make_async_copy(taps_hbm, taps_here, sems.at[1]),
    ]
    for copy in small + mine:
        copy.start()
    small[0].wait()
    conv_turned_ref[...] = conv_here[...].astype(F32).T
    small[1].wait()
    halves = []
    for start in range(0, width, LANES):
        tile = taps_here[:, start : start + LANES]
        halves += [tile, pltpu.roll(tile, LANES // 2, 1)]
    taps = jnp.concatenate(halves, axis=0).T[:peers]
    high = upper(taps)
    taps_ref[0] = high
    taps_ref[1] = taps - high
    total = None
    step = chips // 2
    for start in range(0, chips, step):
        some = range(start, start + step)
        for chip in some:
            mine[chip].wait()
        rows = jnp.concatenate([mine_ref[chip] for chip in some], axis=1)
        part = weight_mine[:, start * depth : (start + step) * depth]
        term = lax.dot_general(rows, part, NT, preferred_element_type=F32)
        total = term if total is None else total + term
    part_ref[...] = total


def second_body(
    group, core_ref, other_ref, part_ref, weight_ref, gate_ref, conv_out_ref, conv_turned_ref, taps_ref,
    grad_gate_ref, out_ref, rows_ref,
):
    chips, _, depth = other_ref.shape
    peers = rows_ref.shape[0] // IN_ROWS
    rows = jnp.concatenate([other_ref[chip] for chip in range(chips)], axis=1)
    starts = [pl.multiple_of((2 * chip + 1 - core_ref[0]) * depth, depth) for chip in range(chips)]
    weight = jnp.concatenate([weight_ref[:, pl.ds(start, depth)] for start in starts], axis=1)
    dmix = part_ref[...] + lax.dot_general(rows, weight, NT, preferred_element_type=F32)
    grad_gate_ref[...] = (dmix * conv_out_ref[...].astype(F32)).astype(BF16)
    signal = upper(gate_ref[...].astype(F32) * dmix).T
    for j in range(group):
        rows_ref[pl.ds(j, peers, stride=IN_ROWS), :] = conv_turned_ref[j * peers : (j + 1) * peers]
        rows_ref[pl.ds(group + 2 + j, peers, stride=IN_ROWS), :] = signal[j * peers : (j + 1) * peers]
    rows_ref[pl.ds(group, peers, stride=IN_ROWS), :] = taps_ref[0]
    rows_ref[pl.ds(group + 1, peers, stride=IN_ROWS), :] = taps_ref[1]
    out_ref[...] = rows_ref[...].astype(BF16)


def conv_body(
    group, blocks, skip_ref, place_ref, in_ref, out_ref,
    in_rows, padded, moved_rows, spans, taps_spans, out_rows, table,
):
    peers = in_rows.shape[0] // IN_ROWS
    parts = LANES // PART
    in_rows[...] = in_ref[...].astype(F32)
    row = lax.broadcasted_iota(jnp.int32, (LANES, LANES), 0)
    lane = lax.broadcasted_iota(jnp.int32, (LANES, LANES), 1)
    flip = (row + lane == LANES - 1).astype(BF16)
    below = (lane < row)[:PART]
    keep = (lane <= row + (LANES - PART))[:PART]
    left = (lane < peers)[:PART]
    rows_lane = lax.broadcasted_iota(jnp.int32, (peers + blocks, LANES), 1)
    tap_lane = lax.broadcasted_iota(jnp.int32, (blocks, LANES), 1) // (LANES // group)
    quarter = LANES // group
    place = place_ref[0]
    tap_rows = []
    for part in range(group):
        high = in_rows[pl.ds(part * IN_ROWS + group, blocks, stride=group * IN_ROWS), :]
        low = in_rows[pl.ds(part * IN_ROWS + group + 1, blocks, stride=group * IN_ROWS), :]
        tap_rows.append(high + low)
    lag_rows = []
    for j in range(group):
        signal = in_rows[pl.ds(group + 2 + j, peers, stride=IN_ROWS), :]
        padded[j, :peers, :] = signal
        padded[j, peers:, :] = jnp.zeros((padded.shape[1] - peers, LANES), F32)
        for a in range(parts):
            if a > 0:
                turned = pltpu.roll(padded[j], LANES - a * PART, 1)
                moved_rows[j] = turned
                here = moved_rows[j, : peers + blocks, :]
                following = moved_rows[j, 1 : peers + blocks + 1, :]
                padded_a = jnp.where(rows_lane < LANES - a * PART, here, following)
                moved_rows[j, : peers + blocks, :] = padded_a
            source = padded if a == 0 else moved_rows
            for k in range(blocks + 1):
                rows = source[j, k : k + peers, :].astype(BF16)
                spans[j, a * peers : (a + 1) * peers, k * LANES : (k + 1) * LANES] = rows
        taps = jnp.zeros((blocks, LANES), F32)
        for part in range(group):
            moved = pltpu.roll(tap_rows[part], (part - j) % group * quarter, 1)
            taps = jnp.where(tap_lane == part, moved, taps)
        before = jnp.zeros((PART, LANES), F32)
        for k in range(blocks + 1):
            if k < blocks:
                spread = jnp.broadcast_to(taps[k : k + 1, :], (PART, LANES))
                now = pltpu.roll(spread, 0, 1, stride=1, stride_axis=0)
            else:
                now = jnp.zeros((PART, LANES), F32)
            both = jnp.where(below, before, now)
            high = both.astype(BF16)
            taps_spans[j, :PART, k * LANES : (k + 1) * LANES] = high
            taps_spans[j, PART:, k * LANES : (k + 1) * LANES] = (both - high.astype(F32)).astype(BF16)
            before = now
    for j in range(group):
        signal = padded[j, :peers, :]
        conv = in_rows[pl.ds(j, peers, stride=IN_ROWS), :].astype(BF16)
        corr = lax.dot_general(taps_spans[j], spans[j], NT, preferred_element_type=F32)
        corr = corr[:PART] + corr[PART:]
        stacked = []
        for a in range(0, parts, 2):
            pair = corr[:, a * peers : (a + 2) * peers]
            stacked += [pair, pltpu.roll(pair, peers, 1)]
        corr = jnp.concatenate(stacked, axis=0).T[:peers]
        gain = skip_ref[j * peers + place]
        out_rows[pl.ds(j, peers, stride=OUT_ROWS), :] = corr + gain * signal
        twice = jnp.concatenate([conv, conv], axis=0)
        turned = lax.dot_general(flip, twice, NT, preferred_element_type=F32)
        pairs = []
        for a in range(0, parts, 2):
            even = turned[LANES - (a + 1) * PART : LANES - a * PART]
            odd = turned[LANES - (a + 2) * PART : LANES - (a + 1) * PART]
            pairs.append(jnp.where(left, even, odd).astype(BF16))
        factors = pairs[0] if len(pairs) == 1 else jnp.concatenate(pairs, axis=1)
        table[j] = jnp.dot(factors, spans[j], preferred_element_type=F32)
    for j in range(group):
        products = table.at[j]
        sums = []
        first = LANES + 1 - PART
        now = pltpu.roll(products[:, :LANES], first, 1, stride=1, stride_axis=0)
        for k in range(blocks):
            tile = products[:, (k + 1) * LANES : (k + 2) * LANES]
            later = pltpu.roll(tile, first, 1, stride=1, stride_axis=0)
            sums.append(jnp.sum(jnp.where(keep, now, later), axis=0, keepdims=True))
            now = later
        lag_rows.append(jnp.concatenate(sums, axis=0))
    for part in range(group):
        mine = jnp.zeros((blocks, LANES), F32)
        for j in range(group):
            moved = pltpu.roll(lag_rows[j], (j - part) % group * quarter, 1)
            mine = jnp.where(tap_lane == j, moved, mine)
        high = upper(mine)
        out_rows[pl.ds(part * OUT_ROWS + group, blocks, stride=group * OUT_ROWS), :] = high
        out_rows[pl.ds(part * OUT_ROWS + group + 1, blocks, stride=group * OUT_ROWS), :] = mine - high
    out_ref[...] = out_rows[...].astype(BF16)


def unpack_body(group, back_ref, grad_input_ref, grad_filter_ref, rows_ref):
    peers = rows_ref.shape[0] // OUT_ROWS
    rows_ref[...] = back_ref[...].astype(F32)
    parts = [rows_ref[pl.ds(j, peers, stride=OUT_ROWS), :] for j in range(group)]
    grad_input_ref[...] = jnp.concatenate(parts, axis=0).T.astype(BF16)
    lags = rows_ref[pl.ds(group, peers, stride=OUT_ROWS), :] + rows_ref[pl.ds(group + 1, peers, stride=OUT_ROWS), :]
    turned = jnp.concatenate([lags, lags], axis=0).T
    quarter = LANES // group
    left = lax.broadcasted_iota(jnp.int32, (quarter, LANES), 1) < peers
    for pair in range(group // 2):
        even = turned[2 * pair * quarter : (2 * pair + 1) * quarter]
        odd = turned[(2 * pair + 1) * quarter : (2 * pair + 2) * quarter]
        grad_filter_ref[:, pair * LANES : (pair + 1) * LANES] = jnp.where(left, even, odd)


def exchange(rows, count):
    peers = lax.axis_size("ctx")
    pairs = rows.reshape(peers, count // 2, 2, rows.shape[1])
    return lax.all_to_all(pairs, "ctx", 0, 0, tiled=True).reshape(rows.shape)


def local(grad_out, out_weight, gate_values, conv_input, conv_output, long_filter, skip_gain):
    tok_rows, chan_width = conv_input.shape
    peers = lax.axis_size("ctx")
    group = chan_width // peers
    lag_rows = long_filter.shape[0]
    blocks = lag_rows * peers // tok_rows
    place = lax.axis_index("ctx").astype(jnp.int32).reshape(1)
    vmem = pltpu.VMEM
    shape = jax.ShapeDtypeStruct
    smem = pl.BlockSpec(memory_space=pltpu.SMEM)
    whole = pl.BlockSpec(memory_space=pltpu.VMEM)

    chips = lax.axis_size("ch") // 2
    core = (lax.axis_index("ch") % 2).astype(jnp.int32).reshape(1)
    core, place = lax.optimization_barrier((core, place))
    sides = [[2 * chip + side for chip in range(chips)] for side in range(2)]
    copies = jnp.broadcast_to(grad_out[None], (chips, tok_rows, chan_width))
    mine = lax.all_to_all(copies, "ch", 0, 0, tiled=True, axis_index_groups=sides)
    other = lax.ppermute(mine, "ch", [(i, i ^ 1) for i in range(2 * chips)])

    hbm = pl.BlockSpec(memory_space=pltpu.HBM)
    dma = pltpu.SemaphoreType.DMA
    half = chips * chan_width
    local_shape = (tok_rows, chan_width)
    stored = (out_weight, conv_input, long_filter)
    part, conv_turned, taps = call(
        functools.partial(first_body, group),
        (
            shape(local_shape, F32),
            shape((chan_width, tok_rows), F32),
            shape((2, peers, tok_rows), F32),
        ),
        [
            vmem((chan_width, half), BF16),
            vmem(local_shape, BF16),
            vmem((lag_rows, chan_width), F32),
            dma((chips,)),
            dma((2,)),
        ],
        tok_rows * out_weight.size,
        2 * out_weight.size,
    )(in_specs=[smem, whole] + [hbm] * 3)(
        core, mine, *(pltpu.with_memory_space_constraint(held, pltpu.HBM) for held in stored)
    )
    grad_gate, rows = call(
        functools.partial(second_body, group),
        (shape(local_shape, BF16), shape((peers * IN_ROWS, tok_rows), BF16)),
        [vmem((peers * IN_ROWS, tok_rows), F32)],
        tok_rows * out_weight.size,
        2 * out_weight.size,
    )(in_specs=[smem] + [whole] * 7)(core, other, part, out_weight, gate_values, conv_output, conv_turned, taps)
    rows = exchange(rows, IN_ROWS)

    span = (blocks + 1) * tok_rows
    back = call(
        functools.partial(conv_body, group, blocks),
        shape((peers * OUT_ROWS, tok_rows), BF16),
        [
            vmem((peers * IN_ROWS, tok_rows), F32),
            vmem((group, peers + blocks + 8, tok_rows), F32),
            vmem((group, peers + blocks + 8, tok_rows), F32),
            vmem((group, peers * (tok_rows // PART), span), BF16),
            vmem((group, 2 * PART, span), BF16),
            vmem((peers * OUT_ROWS, tok_rows), F32),
            vmem((group, PART, span), F32),
        ],
        6 * group * peers * tok_rows * span,
        1_000_000,
    )(in_specs=[smem, smem, whole])(skip_gain, place, rows)
    back = exchange(back, OUT_ROWS)
    grad_input, grad_filter = call(
        functools.partial(unpack_body, group),
        (shape((tok_rows, chan_width), BF16), shape((lag_rows, chan_width), F32)),
        [vmem((peers * OUT_ROWS, tok_rows), F32)],
        0,
        300_000,
    )()(back)
    return grad_input, grad_gate, grad_filter


def solution(mesh):
    in_specs = (
        P("ctx", "ch"),
        P("ch", None),
        P("ctx", "ch"),
        P("ctx", "ch"),
        P("ctx", "ch"),
        P("ctx", "ch"),
        P("ch"),
    )
    out_specs = (P("ctx", "ch"), P("ctx", "ch"), P("ctx", "ch"))
    return jax.shard_map(local, mesh=mesh, in_specs=in_specs, out_specs=out_specs, check_vma=False)
```

```python
import functools

import jax
import jax.numpy as jnp
from jax import lax
from jax.experimental import pallas as pl
from jax.experimental.pallas import tpu as pltpu
from jax.sharding import PartitionSpec as P

F32 = jnp.float32
BF16 = jnp.bfloat16
LANES = 128
PART = 64
NT = (((1,), (1,)), ((), ()))

IN_ROWS = 10
OUT_ROWS = 6


def call(body, out_shape, scratch, flops, nbytes):
    return functools.partial(
        pl.pallas_call,
        body,
        out_shape=out_shape,
        scratch_shapes=scratch,
        compiler_params=pltpu.CompilerParams(vmem_limit_bytes=40 * 1024 * 1024),
        cost_estimate=pl.CostEstimate(flops=flops, bytes_accessed=nbytes, transcendentals=0),
    )


def upper(value):
    return value.astype(BF16).astype(F32)


def first_body(
    group, core_ref, mine_ref, weight_hbm, conv_hbm, taps_hbm, part_ref, conv_turned_ref, taps_ref,
    weight_mine, conv_here, taps_here, mine_sems, sems,
):
    chips, _, depth = mine_ref.shape
    peers = taps_ref.shape[1]
    width = conv_here.shape[1]
    core = core_ref[0]

    def columns(parity, chip, target, sem):
        first = pl.multiple_of((2 * chip + parity) * depth, depth)
        inside = target.at[:, chip * depth : (chip + 1) * depth]
        return pltpu.make_async_copy(weight_hbm.at[:, pl.ds(first, depth)], inside, sem.at[chip])

    mine = [columns(core, chip, weight_mine, mine_sems) for chip in range(chips)]
    small = [
        pltpu.make_async_copy(conv_hbm, conv_here, sems.at[0]),
        pltpu.make_async_copy(taps_hbm, taps_here, sems.at[1]),
    ]
    for copy in small + mine:
        copy.start()
    small[0].wait()
    conv_turned_ref[...] = conv_here[...].astype(F32).T
    small[1].wait()
    halves = []
    for start in range(0, width, LANES):
        tile = taps_here[:, start : start + LANES]
        halves += [tile, pltpu.roll(tile, LANES // 2, 1)]
    taps = jnp.concatenate(halves, axis=0).T[:peers]
    high = upper(taps)
    taps_ref[0] = high
    taps_ref[1] = taps - high
    total = None
    step = chips // 2
    for start in range(0, chips, step):
        some = range(start, start + step)
        for chip in some:
            mine[chip].wait()
        rows = jnp.concatenate([mine_ref[chip] for chip in some], axis=1)
        part = weight_mine[:, start * depth : (start + step) * depth]
        term = lax.dot_general(rows, part, NT, preferred_element_type=F32)
        total = term if total is None else total + term
    part_ref[...] = total


def second_body(
    group, core_ref, other_ref, part_ref, weight_ref, gate_ref, conv_turned_ref, taps_ref,
    dmix_ref, out_ref, rows_ref,
):
    chips, _, depth = other_ref.shape
    peers = rows_ref.shape[0] // IN_ROWS
    rows = jnp.concatenate([other_ref[chip] for chip in range(chips)], axis=1)
    starts = [pl.multiple_of((2 * chip + 1 - core_ref[0]) * depth, depth) for chip in range(chips)]
    weight = jnp.concatenate([weight_ref[:, pl.ds(start, depth)] for start in starts], axis=1)
    dmix = part_ref[...] + lax.dot_general(rows, weight, NT, preferred_element_type=F32)
    dmix_ref[...] = dmix
    signal = upper(gate_ref[...].astype(F32) * dmix).T
    for j in range(group):
        rows_ref[pl.ds(j, peers, stride=IN_ROWS), :] = conv_turned_ref[j * peers : (j + 1) * peers]
        rows_ref[pl.ds(group + 2 + j, peers, stride=IN_ROWS), :] = signal[j * peers : (j + 1) * peers]
    rows_ref[pl.ds(group, peers, stride=IN_ROWS), :] = taps_ref[0]
    rows_ref[pl.ds(group + 1, peers, stride=IN_ROWS), :] = taps_ref[1]
    out_ref[...] = rows_ref[...].astype(BF16)


def conv_body(
    group, blocks, skip_ref, place_ref, in_ref, out_ref,
    in_rows, padded, moved_rows, spans, taps_spans, out_rows, table,
):
    peers = in_rows.shape[0] // IN_ROWS
    parts = LANES // PART
    in_rows[...] = in_ref[...].astype(F32)
    row = lax.broadcasted_iota(jnp.int32, (LANES, LANES), 0)
    lane = lax.broadcasted_iota(jnp.int32, (LANES, LANES), 1)
    flip = (row + lane == LANES - 1).astype(BF16)
    below = (lane < row)[:PART]
    keep = (lane <= row + (LANES - PART))[:PART]
    left = (lane < peers)[:PART]
    rows_lane = lax.broadcasted_iota(jnp.int32, (peers + blocks, LANES), 1)
    tap_lane = lax.broadcasted_iota(jnp.int32, (blocks, LANES), 1) // (LANES // group)
    quarter = LANES // group
    place = place_ref[0]
    tap_rows = []
    for part in range(group):
        high = in_rows[pl.ds(part * IN_ROWS + group, blocks, stride=group * IN_ROWS), :]
        low = in_rows[pl.ds(part * IN_ROWS + group + 1, blocks, stride=group * IN_ROWS), :]
        tap_rows.append(high + low)
    lag_rows = []
    for j in range(group):
        signal = in_rows[pl.ds(group + 2 + j, peers, stride=IN_ROWS), :]
        padded[j, :peers, :] = signal
        padded[j, peers:, :] = jnp.zeros((padded.shape[1] - peers, LANES), F32)
        for a in range(parts):
            if a > 0:
                turned = pltpu.roll(padded[j], LANES - a * PART, 1)
                moved_rows[j] = turned
                here = moved_rows[j, : peers + blocks, :]
                following = moved_rows[j, 1 : peers + blocks + 1, :]
                padded_a = jnp.where(rows_lane < LANES - a * PART, here, following)
                moved_rows[j, : peers + blocks, :] = padded_a
            source = padded if a == 0 else moved_rows
            for k in range(blocks + 1):
                rows = source[j, k : k + peers, :].astype(BF16)
                spans[j, a * peers : (a + 1) * peers, k * LANES : (k + 1) * LANES] = rows
        taps = jnp.zeros((blocks, LANES), F32)
        for part in range(group):
            moved = pltpu.roll(tap_rows[part], (part - j) % group * quarter, 1)
            taps = jnp.where(tap_lane == part, moved, taps)
        before = jnp.zeros((PART, LANES), F32)
        for k in range(blocks + 1):
            if k < blocks:
                spread = jnp.broadcast_to(taps[k : k + 1, :], (PART, LANES))
                now = pltpu.roll(spread, 0, 1, stride=1, stride_axis=0)
            else:
                now = jnp.zeros((PART, LANES), F32)
            both = jnp.where(below, before, now)
            high = both.astype(BF16)
            taps_spans[j, :PART, k * LANES : (k + 1) * LANES] = high
            taps_spans[j, PART:, k * LANES : (k + 1) * LANES] = (both - high.astype(F32)).astype(BF16)
            before = now
    for j in range(group):
        signal = padded[j, :peers, :]
        conv = in_rows[pl.ds(j, peers, stride=IN_ROWS), :].astype(BF16)
        corr = lax.dot_general(taps_spans[j], spans[j], NT, preferred_element_type=F32)
        corr = corr[:PART] + corr[PART:]
        stacked = []
        for a in range(0, parts, 2):
            pair = corr[:, a * peers : (a + 2) * peers]
            stacked += [pair, pltpu.roll(pair, peers, 1)]
        corr = jnp.concatenate(stacked, axis=0).T[:peers]
        gain = skip_ref[j * peers + place]
        out_rows[pl.ds(j, peers, stride=OUT_ROWS), :] = corr + gain * signal
        twice = jnp.concatenate([conv, conv], axis=0)
        turned = lax.dot_general(flip, twice, NT, preferred_element_type=F32)
        pairs = []
        for a in range(0, parts, 2):
            even = turned[LANES - (a + 1) * PART : LANES - a * PART]
            odd = turned[LANES - (a + 2) * PART : LANES - (a + 1) * PART]
            pairs.append(jnp.where(left, even, odd).astype(BF16))
        factors = pairs[0] if len(pairs) == 1 else jnp.concatenate(pairs, axis=1)
        table[j] = jnp.dot(factors, spans[j], preferred_element_type=F32)
    for j in range(group):
        products = table.at[j]
        sums = []
        first = LANES + 1 - PART
        now = pltpu.roll(products[:, :LANES], first, 1, stride=1, stride_axis=0)
        for k in range(blocks):
            tile = products[:, (k + 1) * LANES : (k + 2) * LANES]
            later = pltpu.roll(tile, first, 1, stride=1, stride_axis=0)
            sums.append(jnp.sum(jnp.where(keep, now, later), axis=0, keepdims=True))
            now = later
        lag_rows.append(jnp.concatenate(sums, axis=0))
    for part in range(group):
        mine = jnp.zeros((blocks, LANES), F32)
        for j in range(group):
            moved = pltpu.roll(lag_rows[j], (j - part) % group * quarter, 1)
            mine = jnp.where(tap_lane == j, moved, mine)
        high = upper(mine)
        out_rows[pl.ds(part * OUT_ROWS + group, blocks, stride=group * OUT_ROWS), :] = high
        out_rows[pl.ds(part * OUT_ROWS + group + 1, blocks, stride=group * OUT_ROWS), :] = mine - high
    out_ref[...] = out_rows[...].astype(BF16)


def unpack_body(group, back_ref, grad_input_ref, grad_filter_ref, rows_ref):
    peers = rows_ref.shape[0] // OUT_ROWS
    rows_ref[...] = back_ref[...].astype(F32)
    parts = [rows_ref[pl.ds(j, peers, stride=OUT_ROWS), :] for j in range(group)]
    grad_input_ref[...] = jnp.concatenate(parts, axis=0).T.astype(BF16)
    lags = rows_ref[pl.ds(group, peers, stride=OUT_ROWS), :] + rows_ref[pl.ds(group + 1, peers, stride=OUT_ROWS), :]
    turned = jnp.concatenate([lags, lags], axis=0).T
    quarter = LANES // group
    left = lax.broadcasted_iota(jnp.int32, (quarter, LANES), 1) < peers
    for pair in range(group // 2):
        even = turned[2 * pair * quarter : (2 * pair + 1) * quarter]
        odd = turned[(2 * pair + 1) * quarter : (2 * pair + 2) * quarter]
        grad_filter_ref[:, pair * LANES : (pair + 1) * LANES] = jnp.where(left, even, odd)


def exchange(rows, count):
    peers = lax.axis_size("ctx")
    pairs = rows.reshape(peers, count // 2, 2, rows.shape[1])
    return lax.all_to_all(pairs, "ctx", 0, 0, tiled=True).reshape(rows.shape)


def local(grad_out, out_weight, gate_values, conv_input, conv_output, long_filter, skip_gain):
    tok_rows, chan_width = conv_input.shape
    peers = lax.axis_size("ctx")
    group = chan_width // peers
    lag_rows = long_filter.shape[0]
    blocks = lag_rows * peers // tok_rows
    place = lax.axis_index("ctx").astype(jnp.int32).reshape(1)
    vmem = pltpu.VMEM
    shape = jax.ShapeDtypeStruct
    smem = pl.BlockSpec(memory_space=pltpu.SMEM)
    whole = pl.BlockSpec(memory_space=pltpu.VMEM)

    chips = lax.axis_size("ch") // 2
    core = (lax.axis_index("ch") % 2).astype(jnp.int32).reshape(1)
    core, place = lax.optimization_barrier((core, place))
    sides = [[2 * chip + side for chip in range(chips)] for side in range(2)]
    copies = jnp.broadcast_to(grad_out[None], (chips, tok_rows, chan_width))
    mine = lax.all_to_all(copies, "ch", 0, 0, tiled=True, axis_index_groups=sides)
    other = lax.ppermute(mine, "ch", [(i, i ^ 1) for i in range(2 * chips)])

    hbm = pl.BlockSpec(memory_space=pltpu.HBM)
    dma = pltpu.SemaphoreType.DMA
    half = chips * chan_width
    local_shape = (tok_rows, chan_width)
    stored = (out_weight, conv_input, long_filter)
    part, conv_turned, taps = call(
        functools.partial(first_body, group),
        (
            shape(local_shape, F32),
            shape((chan_width, tok_rows), F32),
            shape((2, peers, tok_rows), F32),
        ),
        [
            vmem((chan_width, half), BF16),
            vmem(local_shape, BF16),
            vmem((lag_rows, chan_width), F32),
            dma((chips,)),
            dma((2,)),
        ],
        tok_rows * out_weight.size,
        2 * out_weight.size,
    )(in_specs=[smem, whole] + [hbm] * 3)(
        core, mine, *(pltpu.with_memory_space_constraint(held, pltpu.HBM) for held in stored)
    )
    dmix, rows = call(
        functools.partial(second_body, group),
        (shape(local_shape, F32), shape((peers * IN_ROWS, tok_rows), BF16)),
        [vmem((peers * IN_ROWS, tok_rows), F32)],
        tok_rows * out_weight.size,
        2 * out_weight.size,
    )(in_specs=[smem] + [whole] * 6)(core, other, part, out_weight, gate_values, conv_turned, taps)
    rows = exchange(rows, IN_ROWS)
    grad_gate = (dmix * conv_output.astype(F32)).astype(BF16)

    span = (blocks + 1) * tok_rows
    back = call(
        functools.partial(conv_body, group, blocks),
        shape((peers * OUT_ROWS, tok_rows), BF16),
        [
            vmem((peers * IN_ROWS, tok_rows), F32),
            vmem((group, peers + blocks + 8, tok_rows), F32),
            vmem((group, peers + blocks + 8, tok_rows), F32),
            vmem((group, peers * (tok_rows // PART), span), BF16),
            vmem((group, 2 * PART, span), BF16),
            vmem((peers * OUT_ROWS, tok_rows), F32),
            vmem((group, PART, span), F32),
        ],
        6 * group * peers * tok_rows * span,
        1_000_000,
    )(in_specs=[smem, smem, whole])(skip_gain, place, rows)
    back = exchange(back, OUT_ROWS)
    grad_input, grad_filter = call(
        functools.partial(unpack_body, group),
        (shape((tok_rows, chan_width), BF16), shape((lag_rows, chan_width), F32)),
        [vmem((peers * OUT_ROWS, tok_rows), F32)],
        0,
        300_000,
    )()(back)
    return grad_input, grad_gate, grad_filter


def solution(mesh):
    in_specs = (
        P("ctx", "ch"),
        P("ch", None),
        P("ctx", "ch"),
        P("ctx", "ch"),
        P("ctx", "ch"),
        P("ctx", "ch"),
        P("ch"),
    )
    out_specs = (P("ctx", "ch"), P("ctx", "ch"), P("ctx", "ch"))
    return jax.shard_map(local, mesh=mesh, in_specs=in_specs, out_specs=out_specs, check_vma=False)
```
